32 devices in a mesh: wide: 8 (over y, x, core), narrow: 4 (over z).
Axes of the slice: x: 2, y: 2, z: 4, core: 2. Of those that a mesh axis runs over, the one named last changes fastest.
Arguments:
- pooled: bfloat16 [16384, 1024], P(('wide', 'narrow')), may hold values from -6 to 6
- cotangent: bfloat16 [16384, 512], P(('wide', 'narrow')), may hold values from -6 to 6
- w_first: bfloat16 [1024, 1024], P('narrow'), may hold values from -0.1875 to 0.1875
- b_first: float32 [1024], replicated, may hold values from -5 to 5
- w_second: bfloat16 [1024, 512], P('narrow'), may hold values from -0.1875 to 0.1875
- counts: bfloat16 [8, 64, 16384], P(None, 'narrow', 'wide'), may hold values from 0 to 3, as said below
- row_ids: int32 [8, 64], P(None, 'narrow'), may hold values from 0 to 63, as said below
- table: float32 [8, 256, 128], P(None, 'narrow'), may hold values from -6 to 6
- accum: float32 [8, 256, 128], P(None, 'narrow'), may hold values from 0.1 to 10
Outputs:
- new_table: float32 [8, 256, 128], P(None, 'narrow')
- new_accum: float32 [8, 256, 128], P(None, 'narrow')
The draws below stay inside these ranges and needn't reach their ends.
Inputs may be any that keep to these rules, and one draw needn't show every extreme that they name: `counts`: each entry is zero where the sample does not look up the active row, else a positive lookup weight. `row_ids`: for each table, the 16 ids of one owner (slots j * 16 to (j + 1) * 16 - 1) are distinct.
All inputs are finite; a program needn't handle non-finite values.
Results may differ from the reference program's by a relative error of at most 0.0038.
Values may be sent and summed in bfloat16 or wider, within the bound.
A program may use at most 128 MiB of HBM per device.

```python
import math
import jax
import jax.numpy as jnp
from jax import lax

TABLES = 8
EMB = 128
INNER = 1024
TOP = 512
ACT = 16
ROWS_DEV = 64
EMB_ALL = 1024
GROUP_BAGS = 2048
SAMPLES = 16384
N_WIDE = 8
N_NARROW = 4


def draw_counts(key, part):
    level_key = jax.random.fold_in(key, 11)
    hit_key = jax.random.fold_in(key, 12)
    value_key = jax.random.fold_in(key, 13)
    shape = (TABLES, N_NARROW * ACT, N_WIDE * GROUP_BAGS)
    levels = jax.random.randint(level_key, (TABLES, N_NARROW * ACT, 1), 0, 4)
    limits = jnp.right_shift(jnp.int32(1024), levels.astype(jnp.int32))
    hits = jax.random.randint(hit_key, shape, 0, 1024) < limits
    values = 0.25 + 2.75 * jax.random.uniform(value_key, shape, jnp.float32)
    return jnp.where(hits, values, jnp.float32(0.0)).astype(jnp.bfloat16)


def pick_rows(subkey):
    return jax.random.permutation(subkey, ROWS_DEV)[:ACT]


def draw_row_ids(key, part):
    keys = jax.random.split(jax.random.fold_in(key, 21), TABLES * N_NARROW)
    picks = jax.vmap(pick_rows)(keys)
    return picks.reshape(TABLES, N_NARROW * ACT).astype(jnp.int32)


def shard_levels(key, shape, pieces, least, high):
    level = 1.0
    for axis_at, blocks in pieces:
        steps = jax.random.uniform(jax.random.fold_in(jax.random.fold_in(key, 6), axis_at), (blocks,), jnp.float32, least / len(pieces), high / len(pieces))
        level = level * jnp.repeat(jnp.exp(steps), shape[axis_at] // blocks).reshape((-1,) + (1,) * (len(shape) - 1 - axis_at))
    return level


def normal_values(rng, extent, scale, bound, shards=(), kind=jnp.bfloat16):
    gain = shard_levels(rng, extent, shards, -0.22, 0.18) if shards else 1.0
    array = jax.random.normal(rng, extent, jnp.float32) * scale * gain
    return jnp.minimum(jnp.maximum(array, -bound), bound).astype(kind)


def setup_inputs(seed: int = 0) -> dict:
    streams_of = jax.random.split(jax.random.key(seed), 10)
    pooled = normal_values(streams_of[0], (SAMPLES, EMB_ALL), 1.0, 6.0, ((0, 32),))
    cotangent = normal_values(streams_of[1], (SAMPLES, TOP), 1.0, 6.0, ((0, 32),))
    w_first = normal_values(streams_of[2], (EMB_ALL, INNER), EMB_ALL ** -0.5, 0.1875, ((0, 4),))
    b_first = normal_values(streams_of[3], (INNER,), 1.0, 5.0, (), jnp.float32)
    w_second = normal_values(streams_of[4], (INNER, TOP), INNER ** -0.5, 0.1875, ((0, 4),))
    counts = draw_counts(jax.random.fold_in(streams_of[9], 71), 0)
    row_ids = draw_row_ids(jax.random.fold_in(streams_of[9], 71), 0)
    table = normal_values(streams_of[7], (TABLES, N_NARROW * ROWS_DEV, EMB), 1.0, 6.0, ((1, 4),), jnp.float32)
    accum = jnp.clip(jnp.exp(math.log(10.0) - 4.6051702 * jax.random.uniform(streams_of[8], (TABLES, N_NARROW * ROWS_DEV, EMB), jnp.float32) ** shard_levels(streams_of[8], (TABLES, N_NARROW * ROWS_DEV, EMB), ((1, 4),), -0.2, 0.2)), 0.1, 10.0)
    return dict(pooled=pooled, cotangent=cotangent, w_first=w_first, b_first=b_first, w_second=w_second, counts=counts, row_ids=row_ids, table=table, accum=accum)


clip_factor = 0.5
learn_rate = 0.05
epsilon = 1e-08

def tower_back(inputs, cotangent, w_first, b_first, w_second):
    hidden_in = jnp.dot(inputs, w_first, preferred_element_type=jnp.float32) + b_first
    back_hidden = lax.dot_general(cotangent, w_second, (((1,), (1,)), ((), ())), preferred_element_type=jnp.float32)
    sigmoid_val = jax.nn.sigmoid(hidden_in)
    slopes = sigmoid_val * (1.0 + hidden_in * (1.0 - sigmoid_val))
    deltas = (back_hidden * slopes).astype(jnp.bfloat16)
    return lax.dot_general(deltas, w_first, (((1,), (1,)), ((), ())), preferred_element_type=jnp.float32).astype(jnp.bfloat16)

def clip_rows(grads, limit):
    norms = jnp.sqrt(lax.optimization_barrier(jnp.sum(grads * grads, axis=-1, keepdims=True)))
    return grads * (limit / jnp.maximum(norms, limit))

def reference(pooled, cotangent, w_first, b_first, w_second, counts, row_ids, table, accum):
    tables = counts.shape[0]
    emb = table.shape[2]
    bags = counts.shape[2] // N_WIDE
    scale = 1.0 / math.sqrt(bags)
    limit = clip_factor * math.sqrt(emb)

    def one_group(group_index):
        offset = group_index * bags
        inputs = lax.dynamic_slice_in_dim(pooled, offset, bags, 0)
        upstream = lax.dynamic_slice_in_dim(cotangent, offset, bags, 0)
        grad_in = tower_back(inputs, upstream, w_first, b_first, w_second)
        lookups = lax.dynamic_slice_in_dim(counts, offset, bags, 2)
        grads = jnp.stack([jnp.dot(lookups[table_no], grad_in[:, table_no * emb:(table_no + 1) * emb], preferred_element_type=jnp.float32) for table_no in range(tables)])
        return clip_rows(grads * scale, limit)
    summed = lax.optimization_barrier(jnp.sum(lax.map(one_group, jnp.arange(N_WIDE, dtype=jnp.int32)), axis=0))
    slots = row_ids.shape[1]
    owners = jnp.arange(slots, dtype=jnp.int32) // ACT
    rows_global = (owners * ROWS_DEV)[None, :] + row_ids
    table_index = jnp.arange(tables, dtype=jnp.int32)[:, None]
    current = table[table_index, rows_global]
    old_acc = accum[table_index, rows_global]
    new_acc = old_acc + summed * summed
    new_rows = current - learn_rate * summed / (jnp.sqrt(new_acc) + epsilon)
    new_table = table.at[table_index, rows_global].set(new_rows)
    new_accum = accum.at[table_index, rows_global].set(new_acc)
    return (new_table, new_accum)
```

```python
import functools
import math

import jax
import jax.numpy as jnp
from jax import lax
from jax.experimental import pallas as pl
from jax.experimental.pallas import tpu as pltpu
from jax.sharding import PartitionSpec as P

MESH = pl.DeviceIdType.MESH
clip_factor = 0.5
learn_rate = 0.05
epsilon = 1e-08
NT = (((1,), (1,)), ((), ()))


def flip(index, bit):
    return index + bit * (1 - 2 * ((index // bit) % 2))


def pieces_of(shard_rows, n_wide):
    pieces = 1
    while n_wide % (2 * pieces) == 0 and shard_rows % (32 * pieces) == 0:
        pieces *= 2
    return pieces


def orders_of(pieces):
    bits = []
    bit = pieces // 2
    while bit:
        bits.append(bit)
        bit //= 2
    swapped = list(bits)
    if len(bits) > 2:
        swapped[0], swapped[1] = bits[1], bits[0]
    return bits, swapped


def tower_kernel(
    n_wide, n_narrow, pieces, scale, limit,
    pooled_hbm, cot_hbm, w1_hbm, w2_hbm, bias_ref, counts_hbm, out_ref,
    pooled, cot, w1, w2, looks, hidden, back, deltas, gsend, grecv, cbuf, crecv, sums,
    local_sem, wsend_sem, wrecv_sem, csend_sem, crecv_sem, gsend_sem, grecv_sem,
    ssend_sem, srecv_sem, asend_sem, arecv_sem,
):
    wide = lax.axis_index("wide")
    narrow = lax.axis_index("narrow")
    shard = w1_hbm.shape[0]
    piece_rows = shard // pieces
    bags = pooled.shape[0]
    inner = w1.shape[1]
    emb = gsend.shape[2]
    tables, slots = looks.shape[1], looks.shape[2]
    rest = n_narrow - 1
    part = wide % pieces
    base = wide - part
    full = (w1, w2)
    shards = (w1_hbm, w2_hbm)
    orders = orders_of(pieces)
    stages = len(orders[0])

    def lane_block(index, size):
        return pl.ds(pl.multiple_of(index * size, size), size)

    def local(step, src, dst):
        return pltpu.make_async_copy(src, dst, local_sem.at[step])

    own_rows = lane_block(narrow, shard)
    locals_ = [
        local(0, pooled_hbm, pooled),
        local(1, w1_hbm, w1.at[own_rows, :]),
        local(2, cot_hbm, cot),
        local(3, w2_hbm, w2.at[own_rows, :]),
        local(4, counts_hbm.at[:, :, lane_block(narrow, bags)], looks.at[narrow]),
    ]
    for copy in locals_:
        copy.start()

    barrier = pltpu.get_barrier_semaphore()
    for d in range(1, n_narrow):
        pl.semaphore_signal(
            barrier, inc=1, device_id={"narrow": (narrow + d) % n_narrow}, device_id_type=MESH
        )
    for d in range(1, n_wide):
        pl.semaphore_signal(
            barrier, inc=1, device_id={"wide": (wide + d) % n_wide}, device_id_type=MESH
        )
    pl.semaphore_wait(barrier, n_narrow + n_wide - 2)

    def remote(src, dst, send, recv, device):
        return pltpu.make_async_remote_copy(
            src_ref=src, dst_ref=dst, send_sem=send, recv_sem=recv,
            device_id=device, device_id_type=MESH,
        )

    sent = []

    def launch(copy):
        copy.start()
        sent.append(copy)

    def rows_at(source, piece):
        return pl.ds(pl.multiple_of(source * shard + piece * piece_rows, piece_rows), piece_rows)

    for d in range(rest):
        target = {"narrow": (narrow + d + 1) % n_narrow}
        for m in range(2):
            launch(remote(
                shards[m].at[lane_block(part, piece_rows), :],
                full[m].at[rows_at(narrow, part), :],
                wsend_sem.at[m, d, 0], wrecv_sem.at[m, d, 0], target,
            ))
    for d in range(rest):
        owner = (narrow + d + 1) % n_narrow
        launch(remote(
            counts_hbm.at[:, :, lane_block(owner, bags)], looks.at[narrow],
            csend_sem.at[d], crecv_sem.at[d], {"narrow": owner},
        ))

    held = [[[part] for _ in range(rest)] for _ in range(2)]

    def stage_arrive(m, d, stage):
        source = (narrow + n_narrow - d - 1) % n_narrow
        if stage == 0:
            new = [part]
            device = {"narrow": source}
        else:
            bit = orders[m][stage - 1]
            new = [flip(q, bit) for q in held[m][d]]
            device = {"wide": base + flip(part, bit)}
        first = 0 if stage == 0 else len(held[m][d])
        for i, q in enumerate(new):
            view = full[m].at[rows_at(source, q), :]
            remote(
                view, view, wsend_sem.at[m, d, first + i], wrecv_sem.at[m, d, first + i], device
            ).wait_recv()
        if stage:
            held[m][d] = held[m][d] + new

    def stage_send(m, d, stage):
        source = (narrow + n_narrow - d - 1) % n_narrow
        bit = orders[m][stage]
        device = {"wide": base + flip(part, bit)}
        first = len(held[m][d])
        for i, q in enumerate(held[m][d]):
            view = full[m].at[rows_at(source, q), :]
            launch(remote(
                view, view, wsend_sem.at[m, d, first + i], wrecv_sem.at[m, d, first + i], device
            ))

    tile = min(256, inner)

    def add_chunk(source, fresh):
        rows = lane_block(source, shard)
        lhs = pooled[:, rows]

        def body(t, carry):
            columns = lane_block(t, tile)
            value = jnp.dot(lhs, w1[rows, columns], preferred_element_type=jnp.float32)
            if fresh:
                hidden[:, columns] = value
            else:
                hidden[:, columns] = hidden[:, columns] + value
            return carry

        lax.fori_loop(0, inner // tile, body, 0)
        back[:, rows] = lax.dot_general(
            cot[...], w2[rows, :], NT, preferred_element_type=jnp.float32
        )

    chunked = shard % 128 == 0
    for copy in locals_:
        copy.wait()
    if chunked:
        add_chunk(narrow, True)
    for t in range(rest + stages):
        for stage in range(stages + 1):
            d = t - stage
            if 0 <= d < rest:
                for m in range(2):
                    stage_arrive(m, d, stage)
                    if stage < stages:
                        stage_send(m, d, stage)
        d = t - stages
        if chunked and 0 <= d < rest:
            add_chunk((narrow + n_narrow - d - 1) % n_narrow, False)

    def activate(t, carry):
        columns = lane_block(t, tile)
        if chunked:
            value = hidden[:, columns]
            back_value = back[:, columns]
        else:
            value = jnp.dot(pooled[...], w1[:, columns], preferred_element_type=jnp.float32)
            back_value = lax.dot_general(
                cot[...], w2[columns, :], NT, preferred_element_type=jnp.float32
            )
        value = value + bias_ref[:, columns]
        sig = jax.nn.sigmoid(value)
        slopes = sig * (1.0 + value * (1.0 - sig))
        deltas[:, columns] = (back_value * slopes).astype(jnp.bfloat16)
        return carry

    lax.fori_loop(0, inner // tile, activate, 0)

    for d in range(rest):
        source = (narrow + n_narrow - d - 1) % n_narrow
        view = looks.at[source]
        remote(view, view, csend_sem.at[d], crecv_sem.at[d], {"narrow": source}).wait_recv()

    group = max(1, 256 // emb)
    groups = tables // group
    for t in range(groups):
        wrows = w1[t * group * emb:(t + 1) * group * emb, :]
        grad_in = lax.dot_general(
            deltas[...], wrows, NT, preferred_element_type=jnp.float32
        ).astype(jnp.bfloat16)
        for i in range(group):
            k = t * group + i
            lookups = looks[:, k].reshape(n_narrow * slots, bags)
            value = jnp.dot(
                lookups, grad_in[:, i * emb:(i + 1) * emb], preferred_element_type=jnp.float32
            )
            for owner in range(n_narrow):
                gsend[owner, k * slots:(k + 1) * slots, :] = value[owner * slots:(owner + 1) * slots]
        block = pl.ds(t * group * slots, group * slots)
        for d in range(rest):
            owner = (narrow + d + 1) % n_narrow
            launch(remote(
                gsend.at[owner, block, :], grecv.at[narrow, block, :],
                gsend_sem.at[d, t], grecv_sem.at[d, t], {"narrow": owner},
            ))
    total = gsend[narrow]
    for d in range(rest):
        source = (narrow + n_narrow - d - 1) % n_narrow
        for t in range(groups):
            view = grecv.at[source, pl.ds(t * group * slots, group * slots), :]
            remote(view, view, gsend_sem.at[d, t], grecv_sem.at[d, t], {"narrow": source}).wait_recv()
        total = total + grecv[source]
    grads = total * scale
    norms = jnp.sqrt(jnp.sum(grads * grads, axis=-1, keepdims=True))
    clipped = grads * (limit / jnp.maximum(norms, limit))
    span = cbuf.shape[1]
    for i in range(n_wide):
        cbuf[i] = clipped[i * span:(i + 1) * span]
    for e in range(n_wide - 1):
        target = (wide + e + 1) % n_wide
        launch(remote(
            cbuf.at[target], crecv.at[wide], ssend_sem.at[e], srecv_sem.at[e], {"wide": target}
        ))
    summed = cbuf[wide]
    for e in range(n_wide - 1):
        source = (wide + n_wide - e - 1) % n_wide
        view = crecv.at[source]
        remote(view, view, ssend_sem.at[e], srecv_sem.at[e], {"wide": source}).wait_recv()
        summed = summed + crecv[source]
    sums[wide] = summed
    for e in range(n_wide - 1):
        target = (wide + e + 1) % n_wide
        launch(remote(
            sums.at[wide], sums.at[wide], asend_sem.at[e], arecv_sem.at[e], {"wide": target}
        ))
    for e in range(n_wide - 1):
        source = (wide + n_wide - e - 1) % n_wide
        view = sums.at[source]
        remote(view, view, asend_sem.at[e], arecv_sem.at[e], {"wide": source}).wait_recv()
    out_ref[...] = sums[...]
    for copy in sent:
        copy.wait_send()


def update_kernel(ids_ref, summed_ref, table_ref, accum_ref, new_table_ref, new_accum_ref):
    tables, slots = ids_ref.shape
    new_table_ref[...] = table_ref[...]
    new_accum_ref[...] = accum_ref[...]
    for k in range(tables):
        for a in range(slots):
            row = pl.ds(ids_ref[k, a], 1)
            value = summed_ref[k * slots + a:k * slots + a + 1, :]
            grown = accum_ref[k, row, :] + value * value
            new_accum_ref[k, row, :] = grown
            new_table_ref[k, row, :] = table_ref[k, row, :] - learn_rate * value / (
                jnp.sqrt(grown) + epsilon
            )


def shards(n_wide, n_narrow, pooled, cotangent, w_first, b_first, w_second, counts, row_ids, table, accum):
    tables, slots, group_bags = counts.shape
    emb = table.shape[2]
    bags, emb_all = pooled.shape
    shard, inner = w_first.shape
    top = w_second.shape[1]
    pieces = pieces_of(shard, n_wide)
    rows = tables * slots
    span = rows // n_wide
    rest = n_narrow - 1
    groups = tables // max(1, 256 // emb)
    scale = 1.0 / math.sqrt(group_bags)
    limit = clip_factor * math.sqrt(emb)
    hbm = pl.BlockSpec(memory_space=pl.ANY)
    vmem = pl.BlockSpec(memory_space=pltpu.VMEM)
    dma = pltpu.SemaphoreType.DMA
    summed = pl.pallas_call(
        functools.partial(tower_kernel, n_wide, n_narrow, pieces, scale, limit),
        out_shape=jax.ShapeDtypeStruct((n_wide, span, emb), jnp.float32),
        in_specs=[hbm, hbm, hbm, hbm, vmem, hbm],
        out_specs=vmem,
        scratch_shapes=[
            pltpu.VMEM((bags, emb_all), jnp.bfloat16),
            pltpu.VMEM((bags, top), jnp.bfloat16),
            pltpu.VMEM((emb_all, inner), jnp.bfloat16),
            pltpu.VMEM((inner, top), jnp.bfloat16),
            pltpu.VMEM((n_narrow, tables, slots, bags), jnp.bfloat16),
            pltpu.VMEM((bags, inner), jnp.float32),
            pltpu.VMEM((bags, inner), jnp.float32),
            pltpu.VMEM((bags, inner), jnp.bfloat16),
            pltpu.VMEM((n_narrow, rows, emb), jnp.float32),
            pltpu.VMEM((n_narrow, rows, emb), jnp.float32),
            pltpu.VMEM((n_wide, span, emb), jnp.float32),
            pltpu.VMEM((n_wide, span, emb), jnp.float32),
            pltpu.VMEM((n_wide, span, emb), jnp.float32),
            dma((5,)),
            dma((2, rest, pieces)),
            dma((2, rest, pieces)),
            dma((rest,)),
            dma((rest,)),
            dma((rest, groups)),
            dma((rest, groups)),
            dma((n_wide - 1,)),
            dma((n_wide - 1,)),
            dma((n_wide - 1,)),
            dma((n_wide - 1,)),
        ],
        compiler_params=pltpu.CompilerParams(
            collective_id=0, has_side_effects=True, vmem_limit_bytes=56 * 1024 * 1024
        ),
        name="tower",
    )(pooled, cotangent, w_first, w_second, b_first.reshape(1, inner), counts)
    return pl.pallas_call(
        update_kernel,
        out_shape=(
            jax.ShapeDtypeStruct(table.shape, table.dtype),
            jax.ShapeDtypeStruct(accum.shape, accum.dtype),
        ),
        in_specs=[pl.BlockSpec(memory_space=pltpu.SMEM), vmem, vmem, vmem],
        out_specs=(vmem, vmem),
        name="update",
    )(row_ids, summed.reshape(rows, emb), table, accum)


def solution(mesh):
    in_specs = (
        P(("wide", "narrow"), None),
        P(("wide", "narrow"), None),
        P("narrow", None),
        P(),
        P("narrow", None),
        P(None, "narrow", "wide"),
        P(None, "narrow"),
        P(None, "narrow", None),
        P(None, "narrow", None),
    )
    out_specs = (P(None, "narrow", None), P(None, "narrow", None))
    step = functools.partial(shards, mesh.shape["wide"], mesh.shape["narrow"])
    return jax.shard_map(step, mesh=mesh, in_specs=in_specs, out_specs=out_specs, check_vma=False)
```

```python
import functools
import math

import jax
import jax.numpy as jnp
from jax import lax
from jax.experimental import pallas as pl
from jax.experimental.pallas import tpu as pltpu
from jax.sharding import PartitionSpec as P

MESH = pl.DeviceIdType.MESH
clip_factor = 0.5
learn_rate = 0.05
epsilon = 1e-08
skew = 3
NT = (((1,), (1,)), ((), ()))


def flip(index, bit):
    return index + bit * (1 - 2 * ((index // bit) % 2))


def pieces_of(shard_rows, n_wide):
    pieces = 1
    while n_wide % (2 * pieces) == 0 and shard_rows % (32 * pieces) == 0:
        pieces *= 2
    return pieces


def masks_of(pieces):
    across = list(range(2, pieces, 2))
    return [masks for masks in (across, [1] if pieces > 1 else []) if masks]


def flips(index, mask):
    bit = 1
    while bit <= mask:
        if mask & bit:
            index = flip(index, bit)
        bit *= 2
    return index


def tower_kernel(
    n_wide, n_narrow, pieces, scale, limit,
    pooled_hbm, cot_hbm, w1_hbm, w2_hbm, bias_ref, counts_hbm, out_ref,
    pooled, cot, w1, w2, looks, hidden, back, deltas, gfull, gsend, grecv, sums,
    local_sem, wsend_sem, wrecv_sem, csend_sem, crecv_sem, gsend_sem, grecv_sem,
    asend_sem, arecv_sem,
):
    wide = lax.axis_index("wide")
    narrow = lax.axis_index("narrow")
    shard = w1_hbm.shape[0]
    piece_rows = shard // pieces
    bags = pooled.shape[0]
    inner = w1.shape[1]
    emb = gfull.shape[3]
    tables, slots = looks.shape[1], looks.shape[2]
    rest = n_narrow - 1
    part = wide % pieces
    base = wide - part
    masks = masks_of(pieces)
    half = inner // 2
    units = [
        (w1, w1_hbm, pl.ds(0, half)),
        (w1, w1_hbm, pl.ds(half, half)),
        (w2, w2_hbm, pl.ds(0, w2.shape[1])),
    ]
    stages = len(masks)

    def lane_block(index, size):
        return pl.ds(pl.multiple_of(index * size, size), size)

    def local(step, src, dst):
        return pltpu.make_async_copy(src, dst, local_sem.at[step])

    own_rows = lane_block(narrow, shard)
    locals_ = [
        local(0, pooled_hbm, pooled),
        local(1, w1_hbm, w1.at[own_rows, :]),
        local(2, cot_hbm, cot),
        local(3, w2_hbm, w2.at[own_rows, :]),
        local(4, counts_hbm.at[:, :, lane_block(narrow, bags)], looks.at[narrow]),
    ]
    for copy in locals_:
        copy.start()

    barrier = pltpu.get_barrier_semaphore()
    for d in range(1, n_narrow):
        pl.semaphore_signal(
            barrier, inc=1, device_id={"narrow": (narrow + d) % n_narrow}, device_id_type=MESH
        )
    for d in range(1, n_wide):
        pl.semaphore_signal(
            barrier, inc=1, device_id={"wide": (wide + d) % n_wide}, device_id_type=MESH
        )
    pl.semaphore_wait(barrier, n_narrow + n_wide - 2)

    def remote(src, dst, send, recv, device):
        return pltpu.make_async_remote_copy(
            src_ref=src, dst_ref=dst, send_sem=send, recv_sem=recv,
            device_id=device, device_id_type=MESH,
        )

    sent = []

    def launch(copy):
        copy.start()
        sent.append(copy)

    def rows_at(source, piece):
        return pl.ds(pl.multiple_of(source * shard + piece * piece_rows, piece_rows), piece_rows)

    for d in range(rest):
        target = {"narrow": (narrow + d + 1) % n_narrow}
        for u, (ref, shard_ref, columns) in enumerate(units):
            launch(remote(
                shard_ref.at[lane_block(part, piece_rows), columns],
                ref.at[rows_at(narrow, part), columns],
                wsend_sem.at[u, d, 0], wrecv_sem.at[u, d, 0], target,
            ))
    for d in range(rest):
        owner = (narrow + d + 1) % n_narrow
        launch(remote(
            counts_hbm.at[:, :, lane_block(owner, bags)], looks.at[narrow],
            csend_sem.at[d], crecv_sem.at[d], {"narrow": owner},
        ))

    held = [[[part] for _ in range(rest)] for _ in units]

    def stage_arrive(u, d, stage):
        source = (narrow + n_narrow - d - 1) % n_narrow
        ref, _, columns = units[u]
        if stage == 0:
            moves = [(part, {"narrow": source})]
            first = 0
        else:
            moves = [
                (flips(q, mask), {"wide": base + flips(part, mask)})
                for mask in masks[stage - 1] for q in held[u][d]
            ]
            first = len(held[u][d])
        for i, (q, device) in enumerate(moves):
            view = ref.at[rows_at(source, q), columns]
            remote(
                view, view, wsend_sem.at[u, d, first + i], wrecv_sem.at[u, d, first + i], device
            ).wait_recv()
        if stage:
            held[u][d] = held[u][d] + [q for q, _ in moves]

    def stage_send(u, d, stage):
        source = (narrow + n_narrow - d - 1) % n_narrow
        ref, _, columns = units[u]
        slot = len(held[u][d])
        for mask in masks[stage]:
            for q in held[u][d]:
                view = ref.at[rows_at(source, q), columns]
                launch(remote(
                    view, view, wsend_sem.at[u, d, slot], wrecv_sem.at[u, d, slot],
                    {"wide": base + flips(part, mask)},
                ))
                slot += 1

    tile = min(256, inner)

    def add_chunk(source, fresh):
        rows = lane_block(source, shard)
        lhs = pooled[:, rows]

        def body(t, carry):
            columns = lane_block(t, tile)
            value = jnp.dot(lhs, w1[rows, columns], preferred_element_type=jnp.float32)
            if fresh:
                hidden[:, columns] = value
            else:
                hidden[:, columns] = hidden[:, columns] + value
            return carry

        lax.fori_loop(0, inner // tile, body, 0)
        back[:, rows] = lax.dot_general(
            cot[...], w2[rows, :], NT, preferred_element_type=jnp.float32
        )

    chunked = shard % 128 == 0
    for copy in locals_:
        copy.wait()
    if chunked:
        add_chunk(narrow, True)
    items = rest * len(units)
    for t in range(items + skew * stages):
        for stage in range(stages + 1):
            item = t - skew * stage
            if 0 <= item < items:
                d, u = divmod(item, len(units))
                stage_arrive(u, d, stage)
                if stage < stages:
                    stage_send(u, d, stage)
                elif chunked and u == len(units) - 1:
                    add_chunk((narrow + n_narrow - d - 1) % n_narrow, False)

    def activate(t, carry):
        columns = lane_block(t, tile)
        if chunked:
            value = hidden[:, columns]
            back_value = back[:, columns]
        else:
            value = jnp.dot(pooled[...], w1[:, columns], preferred_element_type=jnp.float32)
            back_value = lax.dot_general(
                cot[...], w2[columns, :], NT, preferred_element_type=jnp.float32
            )
        value = value + bias_ref[:, columns]
        sig = jax.nn.sigmoid(value)
        slopes = sig * (1.0 + value * (1.0 - sig))
        deltas[:, columns] = (back_value * slopes).astype(jnp.bfloat16)
        return carry

    lax.fori_loop(0, inner // tile, activate, 0)

    for d in range(rest):
        source = (narrow + n_narrow - d - 1) % n_narrow
        view = looks.at[source]
        remote(view, view, csend_sem.at[d], crecv_sem.at[d], {"narrow": source}).wait_recv()

    groups = tables // 2
    for t in range(groups):
        wrows = w1[2 * t * emb:2 * (t + 1) * emb, :]
        grad_in = lax.dot_general(
            deltas[...], wrows, NT, preferred_element_type=jnp.float32
        ).astype(jnp.bfloat16)
        for i in range(2):
            k = 2 * t + i
            lookups = looks[:, k].reshape(n_narrow * slots, bags)
            value = jnp.dot(
                lookups, grad_in[:, i * emb:(i + 1) * emb], preferred_element_type=jnp.float32
            )
            for owner in range(n_narrow):
                rows = value[owner * slots:(owner + 1) * slots]
                gfull[owner, k] = rows
                gsend[owner, k] = rows.astype(jnp.bfloat16)
        block = pl.ds(2 * t, 2)
        for d in range(rest):
            owner = (narrow + d + 1) % n_narrow
            launch(remote(
                gsend.at[owner, block], grecv.at[narrow, block],
                gsend_sem.at[d, t], grecv_sem.at[d, t], {"narrow": owner},
            ))
    for t in range(groups):
        block = pl.ds(2 * t, 2)
        total = gfull[narrow, block]
        for d in range(rest):
            source = (narrow + n_narrow - d - 1) % n_narrow
            view = grecv.at[source, block]
            remote(view, view, gsend_sem.at[d, t], grecv_sem.at[d, t], {"narrow": source}).wait_recv()
            total = total + grecv[source, block].astype(jnp.float32)
        grads = total * scale
        norms = jnp.sqrt(jnp.sum(grads * grads, axis=-1, keepdims=True))
        sums[wide, block] = (grads * (limit / jnp.maximum(norms, limit))).astype(jnp.bfloat16)
        for e in range(n_wide - 1):
            launch(remote(
                sums.at[wide, block], sums.at[wide, block],
                asend_sem.at[t, e], arecv_sem.at[t, e], {"wide": (wide + e + 1) % n_wide},
            ))
    for t in range(groups):
        block = pl.ds(2 * t, 2)
        for e in range(n_wide - 1):
            source = (wide + n_wide - e - 1) % n_wide
            view = sums.at[source, block]
            remote(view, view, asend_sem.at[t, e], arecv_sem.at[t, e], {"wide": source}).wait_recv()
        summed = sums[0, block].astype(jnp.float32)
        for q in range(1, n_wide):
            summed = summed + sums[q, block].astype(jnp.float32)
        out_ref[block] = summed
    for copy in sent:
        copy.wait_send()


def update_kernel(ids_ref, summed_ref, table_ref, accum_ref, new_table_ref, new_accum_ref):
    tables, slots = ids_ref.shape
    new_table_ref[...] = table_ref[...]
    new_accum_ref[...] = accum_ref[...]
    for k in range(tables):
        for a in range(slots):
            row = pl.ds(ids_ref[k, a], 1)
            value = summed_ref[k, a:a + 1, :]
            grown = accum_ref[k, row, :] + value * value
            new_accum_ref[k, row, :] = grown
            new_table_ref[k, row, :] = table_ref[k, row, :] - learn_rate * value / (
                jnp.sqrt(grown) + epsilon
            )


def shards(n_wide, n_narrow, pooled, cotangent, w_first, b_first, w_second, counts, row_ids, table, accum):
    tables, slots, group_bags = counts.shape
    emb = table.shape[2]
    bags, emb_all = pooled.shape
    shard, inner = w_first.shape
    top = w_second.shape[1]
    pieces = pieces_of(shard, n_wide)
    rest = n_narrow - 1
    groups = tables // 2
    scale = 1.0 / math.sqrt(group_bags)
    limit = clip_factor * math.sqrt(emb)
    hbm = pl.BlockSpec(memory_space=pl.ANY)
    vmem = pl.BlockSpec(memory_space=pltpu.VMEM)
    dma = pltpu.SemaphoreType.DMA
    summed = pl.pallas_call(
        functools.partial(tower_kernel, n_wide, n_narrow, pieces, scale, limit),
        out_shape=jax.ShapeDtypeStruct((tables, slots, emb), jnp.float32),
        in_specs=[hbm, hbm, hbm, hbm, vmem, hbm],
        out_specs=vmem,
        scratch_shapes=[
            pltpu.VMEM((bags, emb_all), jnp.bfloat16),
            pltpu.VMEM((bags, top), jnp.bfloat16),
            pltpu.VMEM((emb_all, inner), jnp.bfloat16),
            pltpu.VMEM((inner, top), jnp.bfloat16),
            pltpu.VMEM((n_narrow, tables, slots, bags), jnp.bfloat16),
            pltpu.VMEM((bags, inner), jnp.float32),
            pltpu.VMEM((bags, inner), jnp.float32),
            pltpu.VMEM((bags, inner), jnp.bfloat16),
            pltpu.VMEM((n_narrow, tables, slots, emb), jnp.float32),
            pltpu.VMEM((n_narrow, tables, slots, emb), jnp.bfloat16),
            pltpu.VMEM((n_narrow, tables, slots, emb), jnp.bfloat16),
            pltpu.VMEM((n_wide, tables, slots, emb), jnp.bfloat16),
            dma((5,)),
            dma((3, rest, pieces)),
            dma((3, rest, pieces)),
            dma((rest,)),
            dma((rest,)),
            dma((rest, groups)),
            dma((rest, groups)),
            dma((groups, n_wide - 1)),
            dma((groups, n_wide - 1)),
        ],
        compiler_params=pltpu.CompilerParams(
            collective_id=0, has_side_effects=True, vmem_limit_bytes=56 * 1024 * 1024
        ),
        name="tower",
    )(pooled, cotangent, w_first, w_second, b_first.reshape(1, inner), counts)
    return pl.pallas_call(
        update_kernel,
        out_shape=(
            jax.ShapeDtypeStruct(table.shape, table.dtype),
            jax.ShapeDtypeStruct(accum.shape, accum.dtype),
        ),
        in_specs=[pl.BlockSpec(memory_space=pltpu.SMEM), vmem, vmem, vmem],
        out_specs=(vmem, vmem),
        name="update",
    )(row_ids, summed, table, accum)


def solution(mesh):
    in_specs = (
        P(("wide", "narrow"), None),
        P(("wide", "narrow"), None),
        P("narrow", None),
        P(),
        P("narrow", None),
        P(None, "narrow", "wide"),
        P(None, "narrow"),
        P(None, "narrow", None),
        P(None, "narrow", None),
    )
    out_specs = (P(None, "narrow", None), P(None, "narrow", None))
    step = functools.partial(shards, mesh.shape["wide"], mesh.shape["narrow"])
    return jax.shard_map(step, mesh=mesh, in_specs=in_specs, out_specs=out_specs, check_vma=False)
```
